32 devices in a mesh: tile: 8 (over z, y), cplx: 4 (over x, core).
Axes of the slice: x: 2, y: 2, z: 4, core: 2. Of those that a mesh axis runs over, the one named last changes fastest.
Arguments:
- pair_tiles: bfloat16 [96, 128, 128, 128], P(('tile', 'cplx'))
- tile_map: int32 [96, 3], replicated, may hold values from -1 to 3, as said below
- lengths: int32 [4], replicated, may hold values from 256 to 512
- resolved: int32 [4, 512], replicated, may hold values 0 or 1
- ln_gain: float32 [128], replicated, may hold values from 0.1 to 1.9
- w_in: bfloat16 [128, 512], replicated, may hold values from -0.5 to 0.5
- w_out: bfloat16 [512, 128], replicated, may hold values from -0.25 to 0.25
- w_head: bfloat16 [128, 64], replicated
- head_bias: float32 [64], replicated, may hold values from -4 to 4
Outputs:
- error_map: float32 [4, 512, 512], P('cplx', 'tile')
- residue_error: float32 [4, 512], P('cplx', 'tile')
- tm_score: float32 [4], P('cplx')
The draws below stay inside these ranges and needn't reach their ends.
Inputs may be any that keep to these rules, and one draw needn't show every extreme that they name: `tile_map`: row (t * 4 + c) * 3 + j is slot j of the device at tile index t and cplx index c and holds the complex, block row and block column of its tile, or -1 three times where the slot is empty. Each tile (k, r, q) with r and q below ceil(lengths[k] / 128) is held by exactly one slot and no other tile is held. Complex k is owned by cplx index k // 1; no two filled slots of one device have the same owner, and for fixed t and j the owners over the 4 cplx indices are all different.
All inputs are finite; a program needn't handle non-finite values.
Results may differ from the reference program's by a relative error of at most 0.0089.
Values sent between devices are 32-bit elements; how exact they have to be, the bound alone decides.
No kernel may reach another device: no remote copies, remote signals or barrier semaphores. Data moves between devices by JAX's collectives and lax.ppermute only.
A program may use at most 128 MiB of HBM per device.

```python
import math
import jax
import jax.numpy as jnp
from jax import lax

C = 128
HID = 512
BINS = 64
TILE = 128
BLOCKS = 4
TILES_DEV = 3
MAXRES = 512
COMPLEXES = 4
TILES = 96
N_TILE = 8
N_CPLX = 4


def draw_pair_tiles(key, part):
    shape = (TILES, TILE, TILE, C)
    base = jax.random.normal(jax.random.fold_in(key, 3), shape, jnp.float32)
    top_scale = math.sqrt(10.0)
    row_scale = jnp.exp(jax.random.uniform(jax.random.fold_in(key, 5), (TILES, TILE, 1, 1), jnp.float32, 0.0, math.log(top_scale)))
    col_scale = jnp.exp(jax.random.uniform(jax.random.fold_in(key, 7), (TILES, 1, TILE, 1), jnp.float32, 0.0, math.log(top_scale)))
    return (base * row_scale * col_scale).astype(jnp.bfloat16)


def draw_w_head(key, part):
    base = jax.random.normal(jax.random.fold_in(key, 9), (C, BINS), jnp.float32)
    return (base * (3.0 / math.sqrt(C))).astype(jnp.bfloat16)


def complex_lengths(key):
    drawn = jax.random.randint(jax.random.fold_in(key, 17), (COMPLEXES,), MAXRES // 2, MAXRES + 1).astype(jnp.int32)
    longest = jax.random.randint(jax.random.fold_in(key, 19), (), 0, COMPLEXES).astype(jnp.int32)
    shortest = (longest + 1) % COMPLEXES
    drawn = drawn.at[shortest].set(MAXRES // 2)
    drawn = drawn.at[longest].set(MAXRES)
    return drawn.astype(jnp.int32)


def draw_lengths(key, part):
    return complex_lengths(key)


def draw_tile_map(key, part):
    lengths = complex_lengths(key)
    block_counts = (lengths + TILE - 1) // TILE
    cpx_dev = COMPLEXES // N_CPLX
    per_owner = N_TILE * TILES_DEV
    row_keys = jax.random.split(jax.random.fold_in(key, 29), N_TILE)
    offsets = jax.vmap(lambda sub_key: jax.random.permutation(sub_key, N_CPLX))(row_keys)[:, :TILES_DEV]
    owner_keys = jax.random.split(jax.random.fold_in(key, 31), N_CPLX)
    owner_ranks = jax.vmap(lambda sub_key: jax.random.permutation(sub_key, per_owner))(owner_keys)
    local_index = jnp.arange(cpx_dev * BLOCKS * BLOCKS, dtype=jnp.int32)
    member = local_index // (BLOCKS * BLOCKS)
    block_row = local_index // BLOCKS % BLOCKS
    block_col = local_index % BLOCKS
    owners = jnp.arange(N_CPLX, dtype=jnp.int32)
    complex_id = owners[:, None] * cpx_dev + member[None, :]
    block_count = block_counts[complex_id]
    is_live = (block_row[None, :] < block_count) & (block_col[None, :] < block_count)
    position = jnp.cumsum(is_live.astype(jnp.int32), axis=1) - 1
    tile_table = jnp.full((N_CPLX, per_owner), -1, jnp.int32)
    tile_table = tile_table.at[jnp.broadcast_to(owners[:, None], is_live.shape), jnp.where(is_live, position, per_owner)].set(jnp.broadcast_to(local_index[None, :], is_live.shape), mode='drop')
    tiles_t = jnp.arange(N_TILE, dtype=jnp.int32)[:, None, None]
    cplx_ids = jnp.arange(N_CPLX, dtype=jnp.int32)[None, :, None]
    slot_ids = jnp.arange(TILES_DEV, dtype=jnp.int32)[None, None, :]
    owner_of = (cplx_ids + offsets[:, None, :]) % N_CPLX
    rank_of = owner_ranks[owner_of, tiles_t * TILES_DEV + slot_ids]
    chosen = tile_table[owner_of, rank_of]
    filled = chosen >= 0
    safe_pick = jnp.maximum(chosen, 0)
    result = jnp.stack([jnp.where(filled, owner_of * cpx_dev + safe_pick // (BLOCKS * BLOCKS), -1), jnp.where(filled, safe_pick // BLOCKS % BLOCKS, -1), jnp.where(filled, safe_pick % BLOCKS, -1)], axis=-1)
    return result.reshape(N_TILE * N_CPLX * TILES_DEV, 3).astype(jnp.int32)


def set_ends(values, stream_key, smallest, top_value):
    longest = values.shape.index(max(values.shape))
    spots = []
    for shift in (0, 1):
        where = [jax.random.randint(jax.random.fold_in(stream_key, axis), (), 0, length) for axis, length in enumerate(values.shape)]
        where[longest] = (where[longest] + shift) % values.shape[longest]
        spots.append(tuple(where))
    return values.at[spots[0]].set(smallest).at[spots[1]].set(top_value)


def bell_draw(rng, shape, width, limit, kind=jnp.bfloat16):
    array = width * jax.random.normal(rng, shape, jnp.float32)
    return jnp.clip(array, min=-limit, max=limit).astype(kind)


def setup_inputs(seed: int = 0) -> dict:
    streams_of = jax.random.split(jax.random.key(seed), 10)
    return {
        "pair_tiles": draw_pair_tiles(jax.random.fold_in(streams_of[9], 71), 0),
        "tile_map": draw_tile_map(jax.random.fold_in(streams_of[9], 71), 0),
        "lengths": draw_lengths(jax.random.fold_in(streams_of[9], 71), 0),
        "resolved": set_ends((jax.random.randint(streams_of[3], (COMPLEXES, MAXRES), 0, 8) < 7).astype(jnp.int32), jax.random.fold_in(streams_of[3], 1), 0, 1),
        "ln_gain": jnp.clip(1.0 + 0.18 * jax.random.normal(streams_of[4], (C,), jnp.float32), 0.1, 1.9),
        "w_in": bell_draw(streams_of[5], (C, HID), C ** -0.5, 0.5),
        "w_out": bell_draw(streams_of[6], (HID, C), HID ** -0.5, 0.25),
        "w_head": draw_w_head(jax.random.fold_in(streams_of[9], 71), 0),
        "head_bias": bell_draw(streams_of[8], (BINS,), 1.0, 4.0, jnp.float32),
    }


EPS = 1e-05

def bin_centers(bin_count):
    bin_step = 31.0 / (bin_count - 2)
    return (jnp.arange(bin_count, dtype=jnp.float32) + 0.5) * bin_step

def d_zero(length):
    clipped = jnp.maximum(length, 19).astype(jnp.float32)
    return 1.24 * jnp.cbrt(clipped - 15.0) - 1.8

def pair_head(row_block, ln_gain, w_in, w_out, w_head, head_bias, centers, distance):
    values = row_block.astype(jnp.float32)
    row_mean = lax.optimization_barrier(jnp.mean(values, axis=-1, keepdims=True))
    centred = values - row_mean
    variance = lax.optimization_barrier(jnp.mean(centred * centred, axis=-1, keepdims=True))
    normed = (centred * lax.rsqrt(variance + EPS) * ln_gain).astype(jnp.bfloat16)
    hidden = jax.nn.relu(jnp.dot(normed, w_in, preferred_element_type=jnp.float32)).astype(jnp.bfloat16)
    updated = (values + jnp.dot(hidden, w_out, preferred_element_type=jnp.float32)).astype(jnp.bfloat16)
    logits = jnp.dot(updated, w_head, preferred_element_type=jnp.float32) + head_bias
    bin_probs = jax.nn.softmax(logits, axis=-1)
    expected = lax.optimization_barrier(jnp.sum(bin_probs * centers, axis=-1))
    tm_term = lax.optimization_barrier(jnp.sum(bin_probs / (1.0 + (centers / distance) ** 2), axis=-1))
    return (expected, tm_term)

def reference(pair_tiles, tile_map, lengths, resolved, ln_gain, w_in, w_out, w_head, head_bias):
    centers = bin_centers(BINS)
    positions = jnp.arange(MAXRES, dtype=jnp.int32)
    valid_mask = ((positions[None, :] < lengths[:, None]) & (resolved > 0)).astype(jnp.float32)

    def visit_slot(carry_state, slot_item):
        error_map, score_rows = carry_state
        one_tile, slot_meta = slot_item
        present = slot_meta[0] >= 0
        complex_id = jnp.maximum(slot_meta[0], 0).astype(jnp.int32)
        block_row = jnp.maximum(slot_meta[1], 0).astype(jnp.int32)
        block_col = jnp.maximum(slot_meta[2], 0).astype(jnp.int32)
        distance = d_zero(lengths[complex_id])
        expected, tm_term = pair_head(one_tile.reshape(TILE * TILE, C), ln_gain, w_in, w_out, w_head, head_bias, centers, distance)
        row_valid = lax.dynamic_slice(valid_mask, (complex_id, block_row * TILE), (1, TILE))[0]
        col_valid = lax.dynamic_slice(valid_mask, (complex_id, block_col * TILE), (1, TILE))[0]
        weight = jnp.where(present, row_valid[:, None] * col_valid[None, :], jnp.float32(0.0))
        error_tile = weight * expected.reshape(TILE, TILE)
        score_tile = lax.optimization_barrier(jnp.sum(weight * tm_term.reshape(TILE, TILE), axis=1))
        corner = (complex_id, block_row * TILE, block_col * TILE)
        previous = lax.dynamic_slice(error_map, corner, (1, TILE, TILE))
        error_map = lax.dynamic_update_slice(error_map, previous + error_tile[None], corner)
        row_corner = (complex_id, block_row * TILE)
        previous_rows = lax.dynamic_slice(score_rows, row_corner, (1, TILE))
        score_rows = lax.dynamic_update_slice(score_rows, previous_rows + score_tile[None], row_corner)
        return ((error_map, score_rows), None)
    initial = (jnp.zeros((COMPLEXES, MAXRES, MAXRES), jnp.float32), jnp.zeros((COMPLEXES, MAXRES), jnp.float32))
    (error_map, score_rows), _ = lax.scan(visit_slot, initial, (pair_tiles, tile_map))
    denominator = jnp.maximum(valid_mask * lax.optimization_barrier(jnp.sum(valid_mask, axis=1, keepdims=True)), jnp.float32(1.0))
    residue_error = lax.optimization_barrier(jnp.sum(error_map, axis=2)) / denominator
    tm_score = lax.optimization_barrier(jnp.max(score_rows / denominator, axis=1))
    return (error_map, residue_error, tm_score)
```

```python
import functools
import math

import jax
import jax.numpy as jnp
from jax import lax
from jax.experimental import pallas as pl
from jax.experimental.pallas import tpu as pltpu
from jax.sharding import PartitionSpec as P

EPS = 1e-05
F32 = jnp.float32
BF16 = jnp.bfloat16
LOG2E = math.log2(math.e)
NT = (((1,), (1,)), ((), ()))
HIGHEST = lax.Precision.HIGHEST
GROUP = 4
PAD = 8
VMEM_LIMIT = 50 * 1024 * 1024


def split_bf16(values):
    high = values.astype(BF16)
    return high, (values - high.astype(F32)).astype(BF16)


def own_slots(map_ref, base, slots):
    return [
        (map_ref[base + s, 0], map_ref[base + s, 1], map_ref[base + s, 2]) for s in range(slots)
    ]


def valid_row(resolved_ref, lengths_ref, member, block, side):
    start = block * side
    if not isinstance(start, int):
        start = pl.multiple_of(start, side)
    flags = resolved_ref[:, pl.ds(start, side)]
    here = lax.broadcasted_iota(jnp.int32, flags.shape, 0) == member
    flags = jnp.max(jnp.where(here, flags, 0), axis=0, keepdims=True)
    position = start + lax.broadcasted_iota(jnp.int32, (1, side), 1)
    return ((flags > 0) & (position < lengths_ref[member])).astype(F32)


def head_kernel(
    dims,
    map_ref,
    lengths_ref,
    flags_ref,
    resolved_ref,
    tiles_ref,
    gain_ref,
    w_in_ref,
    w_out_ref,
    w_head_ref,
    bias_ref,
    *rest,
):
    n_cplx, parts, cpx_dev, slots, side, width, hid, bins, rows_each = dims
    outs = rest[: n_cplx * parts]
    (
        tiles,
        first_w,
        second_w,
        bias_tile,
        sum_w,
        hidden,
        direct,
        spread,
        logits,
        sums,
        errors,
        tm_sums,
        order,
        sems,
    ) = rest[n_cplx * parts :]
    tile_index = lax.axis_index("tile")
    cplx_index = lax.axis_index("cplx")
    part_index = lax.rem(tile_index, parts)
    metas = own_slots(map_ref, (tile_index * n_cplx + cplx_index) * slots, slots)
    total = slots * side

    def slot_copy(s):
        return pltpu.make_async_copy(
            tiles_ref.at[s], tiles.at[pl.ds(s * side, side)], sems.at[s]
        )

    for s in range(slots):

        @pl.when(metas[s][0] >= 0)
        def _(s=s):
            slot_copy(s).start()

    count = jnp.int32(0)
    starts = []
    unroll = 8
    for s in range(slots):
        starts.append(count)
        member = jnp.maximum(metas[s][0], 0)
        base = jnp.maximum(metas[s][1], 0) * side
        limit = jnp.where(metas[s][0] >= 0, jnp.minimum(lengths_ref[member] - base, side), 0)
        limit = jnp.maximum(limit, 0)

        def step(g, cnt, s=s, member=member, base=base, limit=limit):
            for u in range(unroll):
                row = g * unroll + u
                order[cnt] = s * side + row
                keep = (flags_ref[member, base + row] > 0) & (row < limit)
                cnt = cnt + keep.astype(jnp.int32)
            return cnt

        count = lax.fori_loop(0, pl.cdiv(limit, unroll), step, count)
    batch = 2 * GROUP
    for u in range(2 * batch):
        order[count + u] = total

    w_in_t = jnp.transpose(w_in_ref[...].astype(F32)) * gain_ref[...]
    w_in_t = w_in_t - jnp.mean(w_in_t, axis=1, keepdims=True)
    head_t = jnp.transpose(w_head_ref[...].astype(F32))
    both = jnp.concatenate([w_in_t, head_t * LOG2E], axis=0)
    high, low = split_bf16(both)
    first_w[: hid + bins, :width] = high
    first_w[: hid + bins, width:] = low
    row_id = lax.broadcasted_iota(jnp.int32, (width, width), 0)
    col_id = lax.broadcasted_iota(jnp.int32, (width, width), 1)
    centring = jnp.where(row_id == col_id, 1.0, 0.0) - 1.0 / width
    first_w[hid + bins :, :width] = centring.astype(BF16)
    first_w[hid + bins :, width:] = jnp.zeros((width, width), BF16)
    second = lax.dot_general(head_t.astype(BF16), w_out_ref[...], NT, preferred_element_type=F32)
    second_w[...] = (second * LOG2E).astype(BF16)
    bias_tile[...] = jnp.transpose(jnp.broadcast_to(bias_ref[...] * LOG2E, (128, bins)))
    step_size = 31.0 / (bins - 2)
    centers = (lax.broadcasted_iota(jnp.int32, (1, bins), 1).astype(F32) + 0.5) * step_size
    sum_rows = [jnp.ones((1, bins), F32).astype(BF16), centers.astype(BF16)]
    for s in range(slots):
        length = lengths_ref[jnp.maximum(metas[s][0], 0)]
        clipped = jnp.full((1, bins), jnp.maximum(length, 19) - 15, jnp.int32).astype(F32)
        distance = 1.24 * jnp.exp(jnp.log(clipped) * (1.0 / 3.0)) - 1.8
        sum_rows.extend(split_bf16(1.0 / (1.0 + (centers / distance) ** 2)))
    extra = sum_w.shape[0] - len(sum_rows)
    if extra:
        sum_rows.append(jnp.zeros((extra, bins), BF16))
    sum_w[...] = jnp.concatenate([r.astype(F32) for r in sum_rows], axis=0).astype(BF16)

    lanes = GROUP * side

    def project(first_row, slot):
        rows = [tiles[order[first_row + u]] for u in range(GROUP)]
        pairs = jnp.concatenate(rows, axis=0)
        pairs = jnp.concatenate([pairs, pairs], axis=1)
        out = lax.dot_general(first_w[...], pairs, NT, preferred_element_type=F32)
        hidden[slot] = jnp.maximum(out[:hid].astype(BF16), 0)
        direct[slot] = out[hid : hid + bins]
        centred = out[hid + bins :]
        variance = jnp.sum(centred * centred, axis=0, keepdims=True) * (1.0 / width)
        spread[slot] = jnp.broadcast_to(lax.rsqrt(variance + EPS), (8, lanes))

    def combine(slot):
        change = jnp.dot(second_w[...], hidden[slot], preferred_element_type=F32)
        scale = spread[slot][:1]
        bias = jnp.concatenate([bias_tile[...]] * (lanes // 128), axis=1)
        logits[slot] = direct[slot] + bias + jnp.where(scale > 0, scale * change, 0.0)

    def reduce(first_row, slot):
        values = logits[slot]
        top = jnp.max(values, axis=0, keepdims=True)
        weights = jnp.exp2(values - top).astype(BF16)
        found = jnp.dot(sum_w[...], weights, preferred_element_type=F32)
        for u in range(GROUP):
            row = order[jnp.maximum(first_row + u, 0)]
            row = jnp.where(first_row + u >= 0, row, total)
            sums[row] = found[:, u * side : (u + 1) * side]

    def wait_slots(first_row, last_row, condition):
        for s in range(slots):

            @pl.when(condition(s))
            def _(s=s):
                slot_copy(s).wait()

    steps = pl.cdiv(count, batch)

    def loop(g, carry):
        row = g * batch
        for s in range(slots):
            begin = starts[s]

            @pl.when((metas[s][0] >= 0) & (begin // batch == g))
            def _(s=s):
                slot_copy(s).wait()

        project(row, 0)
        combine(1)
        reduce(row - 2 * GROUP, 0)
        project(row + GROUP, 1)
        combine(0)
        reduce(row - GROUP, 1)
        return carry

    lax.fori_loop(0, steps + 1, loop, 0)
    for s in range(slots):

        @pl.when((metas[s][0] >= 0) & (starts[s] // batch > steps))
        def _(s=s):
            slot_copy(s).wait()

    for s in range(slots):
        member = jnp.maximum(metas[s][0], 0)
        block_row = jnp.maximum(metas[s][1], 0)
        block_col = jnp.maximum(metas[s][2], 0)
        row_ok = valid_row(resolved_ref, lengths_ref, member, block_row, side)
        col_ok = valid_row(resolved_ref, lengths_ref, member, block_col, side)
        keep_row = lax.broadcasted_iota(jnp.int32, (8, side), 0) == 0
        outer = lax.dot_general(
            jnp.where(keep_row, row_ok, 0.0),
            jnp.where(keep_row, col_ok, 0.0),
            (((0,), (0,)), ((), ())),
            preferred_element_type=F32,
        )
        mass = sums[pl.ds(s * side, side), 0, :]
        inverse = 1.0 / mass
        expected = sums[pl.ds(s * side, side), 1, :] * inverse
        high = sums[pl.ds(s * side, side), 2 + 2 * s, :]
        low = sums[pl.ds(s * side, side), 3 + 2 * s, :]
        errors[s] = jnp.where(outer > 0, expected, 0.0)
        term = jnp.where(outer > 0, (high + low) * inverse, 0.0)
        tm_sums[s] = lax.dot_general(
            jnp.ones((PAD, side), F32), term, NT, preferred_element_type=F32, precision=HIGHEST
        )

    for shift in range(n_cplx):
        owner = lax.rem(cplx_index + shift, n_cplx)
        chosen = jnp.int32(0)
        for s in range(slots):
            hit = (metas[s][0] >= 0) & (metas[s][0] // cpx_dev == owner)
            chosen = jnp.where(hit, s, chosen)
        for part_shift in range(parts):
            part = lax.rem(part_index + part_shift, parts)
            out = outs[shift * parts + part_shift]
            first = pl.multiple_of(part * rows_each, rows_each)
            out[:rows_each] = errors[chosen, pl.ds(first, rows_each)]
            out[rows_each:] = tm_sums[chosen]


def place_kernel(dims, map_ref, *rest):
    n_cplx, parts, cpx_dev, slots, blocks, rows_each, side = dims
    pieces = rest[: n_cplx * parts]
    outs = rest[n_cplx * parts : n_cplx * parts + blocks]
    (tm_rows,) = rest[n_cplx * parts + blocks :]
    tile_index = lax.axis_index("tile")
    cplx_index = lax.axis_index("cplx")
    part_index = lax.rem(tile_index, parts)
    block_index = tile_index // parts
    body = cpx_dev * blocks * rows_each
    for out in outs:
        out[...] = jnp.zeros_like(out)
    tm_rows[...] = jnp.zeros_like(tm_rows)
    for shift in range(n_cplx):
        source = lax.rem(cplx_index + (n_cplx - shift), n_cplx)
        for part_shift in range(parts):
            part = lax.rem(part_index + (parts - part_shift), parts)
            device = (block_index * parts + part) * n_cplx + source
            piece = pieces[shift * parts + part_shift]
            member = jnp.int32(-1)
            block_row = jnp.int32(0)
            block_col = jnp.int32(0)
            for s, (k, r, q) in enumerate(own_slots(map_ref, device * slots, slots)):
                hit = (k >= 0) & (k // cpx_dev == cplx_index)
                member = jnp.where(hit, k - cplx_index * cpx_dev, member)
                block_row = jnp.where(hit, r, block_row)
                block_col = jnp.where(hit, q, block_col)
            offset = lax.rem(block_row - block_index + blocks, blocks)
            for b in range(blocks):

                @pl.when((member >= 0) & (offset == b))
                def _(b=b, piece=piece, member=member, block_col=block_col):
                    first = pl.multiple_of((member * blocks + block_col) * rows_each, 8)
                    outs[b][pl.ds(first, rows_each)] = piece[:rows_each]

            @pl.when(member >= 0)
            def _(piece=piece, member=member, block_row=block_row):
                row = member * blocks + block_row
                tm_rows[pl.ds(row, 1)] += piece[rows_each : rows_each + 1]

    for out in outs:
        out[body:] = tm_rows[...]


def finish_kernel(dims, lengths_ref, resolved_ref, *rest):
    parts, cpx_dev, blocks, rows_each, side = dims
    shares = rest[:blocks]
    map_out, error_out, score_out = rest[blocks:]
    tile_index = lax.axis_index("tile")
    cplx_index = lax.axis_index("cplx")
    part_index = lax.rem(tile_index, parts)
    block_index = tile_index // parts
    body = cpx_dev * blocks * rows_each
    tm_all = shares[0][body:]
    for share in shares[1:]:
        tm_all = tm_all + share[body:]
    for m in range(cpx_dev):
        member = cplx_index * cpx_dev + m
        masks = [valid_row(resolved_ref, lengths_ref, member, b, side) for b in range(blocks)]
        count = jnp.sum(functools.reduce(jnp.add, masks), axis=1, keepdims=True)
        row_sum = jnp.zeros((rows_each, side), F32)
        for q in range(blocks):
            rows = pl.ds((m * blocks + q) * rows_each, rows_each)
            block = shares[0][rows]
            for share in shares[1:]:
                block = block + share[rows]
            map_out[m, :, q * side : (q + 1) * side] = block
            row_sum = row_sum + block
        row_total = lax.dot_general(
            jnp.ones((8, side), F32), row_sum, NT, preferred_element_type=F32, precision=HIGHEST
        )[:1]
        best = jnp.zeros((1, side), F32)
        own_mask = jnp.zeros((1, side), F32)
        for b in range(blocks):
            denominator = jnp.maximum(masks[b] * count, 1.0)
            ratio = tm_all[m * blocks + b : m * blocks + b + 1] / denominator
            best = ratio if b == 0 else jnp.maximum(best, ratio)
            own_mask = jnp.where(block_index == b, masks[b], own_mask)
        own_mask = pltpu.roll(
            jnp.broadcast_to(own_mask, (8, side)),
            lax.rem(side - part_index * rows_each, side),
            axis=1,
        )[:1, :rows_each]
        error_out[m : m + 1, :] = row_total / jnp.maximum(own_mask * count, 1.0)
        score_out[m] = jnp.max(best)


def shards(pair_tiles, tile_map, lengths, resolved, ln_gain, w_in, w_out, w_head, head_bias):
    n_tile = lax.axis_size("tile")
    n_cplx = lax.axis_size("cplx")
    slots, side, _, width = pair_tiles.shape
    complexes, maxres = resolved.shape
    hid = w_in.shape[1]
    bins = w_head.shape[1]
    blocks = maxres // side
    cpx_dev = complexes // n_cplx
    rows_each = maxres // n_tile
    parts = side // rows_each
    smem = pl.BlockSpec(memory_space=pltpu.SMEM)
    vmem = pl.BlockSpec(memory_space=pltpu.VMEM)
    axes = ("tile", "cplx")
    sum_count = -(-(2 + 2 * slots) // 8) * 8
    lanes = GROUP * side

    def move(value, block_shift, part_shift, cplx_shift):
        pairs = []
        for t in range(n_tile):
            to_block = (t // parts + block_shift) % blocks
            to_part = (t % parts + part_shift) % parts
            for c in range(n_cplx):
                to = (to_block * parts + to_part) * n_cplx + (c + cplx_shift) % n_cplx
                pairs.append((t * n_cplx + c, to))
        return lax.ppermute(value, axes, pairs)

    piece = jax.ShapeDtypeStruct((rows_each + PAD, side), F32)
    pieces = pl.pallas_call(
        functools.partial(
            head_kernel, (n_cplx, parts, cpx_dev, slots, side, width, hid, bins, rows_each)
        ),
        out_shape=[piece] * (n_cplx * parts),
        in_specs=[smem, smem, smem, vmem, pl.BlockSpec(memory_space=pl.ANY)] + [vmem] * 5,
        out_specs=[vmem] * (n_cplx * parts),
        scratch_shapes=[
            pltpu.VMEM((slots * side + 8, side, width), BF16),
            pltpu.VMEM((hid + bins + width, 2 * width), BF16),
            pltpu.VMEM((bins, hid), BF16),
            pltpu.VMEM((bins, 128), F32),
            pltpu.VMEM((sum_count, bins), BF16),
            pltpu.VMEM((2, hid, lanes), BF16),
            pltpu.VMEM((2, bins, lanes), F32),
            pltpu.VMEM((2, 8, lanes), F32),
            pltpu.VMEM((2, bins, lanes), F32),
            pltpu.VMEM((slots * side + 8, sum_count, side), F32),
            pltpu.VMEM((slots, side, side), F32),
            pltpu.VMEM((slots, PAD, side), F32),
            pltpu.SMEM((slots * side + 64,), jnp.int32),
            pltpu.SemaphoreType.DMA((slots,)),
        ],
        compiler_params=pltpu.CompilerParams(vmem_limit_bytes=VMEM_LIMIT),
    )(
        tile_map,
        lengths,
        resolved,
        resolved,
        pair_tiles,
        ln_gain.reshape(1, width),
        w_in,
        w_out,
        w_head,
        head_bias.reshape(1, bins),
    )
    moved = []
    for shift in range(n_cplx):
        for part_shift in range(parts):
            value = pieces[shift * parts + part_shift]
            moved.append(move(value, 0, part_shift, shift) if shift or part_shift else value)

    tm_pad = -(-(cpx_dev * blocks) // 8) * 8
    share = jax.ShapeDtypeStruct((cpx_dev * blocks * rows_each + tm_pad, side), F32)
    shares = pl.pallas_call(
        functools.partial(
            place_kernel, (n_cplx, parts, cpx_dev, slots, blocks, rows_each, side)
        ),
        out_shape=[share] * blocks,
        in_specs=[smem] + [vmem] * len(moved),
        out_specs=[vmem] * blocks,
        scratch_shapes=[pltpu.VMEM((tm_pad, side), F32)],
    )(tile_map, *moved)
    arrived = [move(shares[b], b, 0, 0) if b else shares[b] for b in range(blocks)]

    return pl.pallas_call(
        functools.partial(finish_kernel, (parts, cpx_dev, blocks, rows_each, side)),
        out_shape=[
            jax.ShapeDtypeStruct((cpx_dev, rows_each, maxres), F32),
            jax.ShapeDtypeStruct((cpx_dev, rows_each), F32),
            jax.ShapeDtypeStruct((cpx_dev,), F32),
        ],
        in_specs=[smem, vmem] + [vmem] * blocks,
        out_specs=[vmem, vmem, smem],
    )(lengths, resolved, *arrived)


def solution(mesh):
    placed = (P(("tile", "cplx"), None, None, None), P(), P(), P(), P(), P(), P(), P(), P())
    return jax.shard_map(
        shards,
        mesh=mesh,
        in_specs=placed,
        out_specs=(P("cplx", "tile", None), P("cplx", "tile"), P("cplx")),
        check_vma=False,
    )
```

```python
import functools
import math

import jax
import jax.numpy as jnp
from jax import lax
from jax.experimental import pallas as pl
from jax.experimental.pallas import tpu as pltpu
from jax.sharding import PartitionSpec as P

EPS = 1e-05
F32 = jnp.float32
BF16 = jnp.bfloat16
LOG2E = math.log2(math.e)
NT = (((1,), (1,)), ((), ()))
HIGHEST = lax.Precision.HIGHEST
GROUP = 4
UNROLL = 4
MXUS = 2
CHUNK = 64
PAD = 8
VMEM_LIMIT = 67043328


def split_bf16(values):
    high = values.astype(BF16)
    return high, (values - high.astype(F32)).astype(BF16)


def own_slots(map_ref, base, slots):
    return [
        (map_ref[0, base + s], map_ref[1, base + s], map_ref[2, base + s]) for s in range(slots)
    ]


def valid_row(resolved_ref, lengths_ref, member, block, side):
    start = block * side
    if not isinstance(start, int):
        start = pl.multiple_of(start, side)
    flags = resolved_ref[:, pl.ds(start, side)]
    here = lax.broadcasted_iota(jnp.int32, flags.shape, 0) == member
    flags = jnp.max(jnp.where(here, flags, 0), axis=0, keepdims=True)
    position = start + lax.broadcasted_iota(jnp.int32, (1, side), 1)
    return ((flags > 0) & (position < lengths_ref[member])).astype(F32)


def head_body(
    dims,
    map_ref,
    lengths_ref,
    flags_ref,
    resolved_ref,
    tiles_ref,
    gain_ref,
    w_in_ref,
    w_out_ref,
    w_head_ref,
    bias_ref,
    *rest,
):
    n_cplx, parts, cpx_dev, slots, side, width, hid, bins, rows_each = dims
    outs = rest[: n_cplx * parts]
    (
        tiles,
        first_w,
        second_w,
        bias_tile,
        center_tile,
        tm_tile,
        hidden,
        direct,
        spread,
        logits,
        found_error,
        found_term,
        errors,
        tm_sums,
        order,
        sems,
        *accs,
    ) = rest[n_cplx * parts :]
    accs = [accs[m :: MXUS] for m in range(MXUS)]
    tile_index = lax.axis_index("tile")
    cplx_index = lax.axis_index("cplx")
    part_index = lax.rem(tile_index, parts)
    metas = own_slots(map_ref, (tile_index * n_cplx + cplx_index) * slots, slots)
    total = slots * side

    def slot_copy(s):
        return pltpu.make_async_copy(
            tiles_ref.at[s], tiles.at[pl.ds(s * side, side)], sems.at[s]
        )

    for s in range(slots):

        @pl.when(metas[s][0] >= 0)
        def _(s=s):
            slot_copy(s).start()

    count = jnp.int32(0)
    starts = []
    unroll = 8
    for s in range(slots):
        starts.append(count)
        member = jnp.maximum(metas[s][0], 0)
        base = jnp.maximum(metas[s][1], 0) * side
        limit = jnp.where(metas[s][0] >= 0, jnp.minimum(lengths_ref[member] - base, side), 0)
        limit = jnp.maximum(limit, 0)

        def step(g, cnt, s=s, member=member, base=base, limit=limit):
            for u in range(unroll):
                row = g * unroll + u
                order[cnt] = s * side + row
                keep = (flags_ref[member, base + row] > 0) & (row < limit)
                cnt = cnt + keep.astype(jnp.int32)
            return cnt

        count = lax.fori_loop(0, pl.cdiv(limit, unroll), step, count)
    batch = UNROLL * GROUP
    for u in range(4 * GROUP + batch):
        order[count + u] = total

    w_in_t = jnp.transpose(w_in_ref[...].astype(F32)) * gain_ref[...]
    w_in_t = w_in_t - jnp.mean(w_in_t, axis=1, keepdims=True)
    head_t = w_head_ref[...].astype(F32)
    both = jnp.concatenate([w_in_t, head_t * LOG2E], axis=0)
    high, low = split_bf16(both)
    first_w[: hid + bins, :width] = high
    first_w[: hid + bins, width:] = low
    row_id = lax.broadcasted_iota(jnp.int32, (width, width), 0)
    col_id = lax.broadcasted_iota(jnp.int32, (width, width), 1)
    centring = jnp.where(row_id == col_id, 1.0, 0.0) - 1.0 / width
    first_w[hid + bins :, :width] = centring.astype(BF16)
    first_w[hid + bins :, width:] = jnp.zeros((width, width), BF16)
    left = jnp.concatenate([head_t, jnp.zeros_like(head_t)], axis=1).astype(BF16)
    for k in range(hid // (2 * width)):
        part = w_out_ref[k * 2 * width : (k + 1) * 2 * width]
        right = jnp.concatenate([part, jnp.zeros_like(part)], axis=1)
        pltpu.matmul_push_rhs(right, 0, k % MXUS, transpose=True)
        acc = accs[k % MXUS][0]
        pltpu.matmul_acc_lhs(acc, left, 0)
        second = pltpu.matmul_pop(acc) * LOG2E
        second_w[:, k * 2 * width : (k + 1) * 2 * width] = second.astype(BF16)
    bias_tile[...] = jnp.transpose(jnp.broadcast_to(bias_ref[...] * LOG2E, (128, bins)))
    step_size = 31.0 / (bins - 2)
    bin_id = lax.broadcasted_iota(jnp.int32, (bins, 128), 0)
    centers = (bin_id.astype(F32) + 0.5) * step_size
    center_tile[...] = centers
    for s in range(slots):
        length = lengths_ref[jnp.maximum(metas[s][0], 0)]
        clipped = jnp.full((bins, 128), jnp.maximum(length, 19) - 15, jnp.int32).astype(F32)
        distance = 1.24 * jnp.exp(jnp.log(clipped) * (1.0 / 3.0)) - 1.8
        tm_tile[s] = 1.0 / (1.0 + (centers / distance) ** 2)

    lanes = GROUP * side
    half = lanes // MXUS
    depth = 2 * width
    chunks = (hid + bins + width) // CHUNK

    def push_pairs(first_row):
        for m in range(MXUS):
            rows = [tiles[order[first_row + m * (GROUP // MXUS) + u]] for u in range(GROUP // MXUS)]
            pairs = jnp.concatenate(rows, axis=0)
            pairs = jnp.concatenate([pairs, pairs], axis=1)
            pltpu.matmul_push_rhs(pairs, 0, m, transpose=True)

    def take(slot, chunk, m, variance):
        value = pltpu.matmul_pop(accs[m][chunk])
        at = chunk * CHUNK
        cols = slice(m * half, (m + 1) * half)
        if at < hid:
            hidden[slot, at : at + CHUNK, cols] = jnp.maximum(value.astype(BF16), 0)
        elif at < hid + bins:
            direct[slot, at - hid : at - hid + CHUNK, cols] = value
        else:
            part = jnp.sum((value * value).reshape(CHUNK // 8, 8, half), axis=0)
            variance[m] = part if variance[m] is None else variance[m] + part

    def weigh(first_row, slot):
        for u in range(GROUP):
            row = order[jnp.maximum(first_row + u, 0)]
            row = jnp.where(first_row + u >= 0, row, total)
            values = logits[slot, :, u * side : (u + 1) * side]
            top = jnp.max(values, axis=0, keepdims=True)
            weights = jnp.exp2(values - top)
            inverse = 1.0 / jnp.sum(weights, axis=0, keepdims=True)
            expected = jnp.sum(weights * center_tile[...], axis=0, keepdims=True)
            term = jnp.sum(weights * tm_tile[row // side], axis=0, keepdims=True)
            found_error[pl.ds(row, 1)] = expected * inverse
            found_term[pl.ds(row, 1)] = term * inverse

    def stage(group, slot):
        other = 1 - slot
        variance = [None] * MXUS
        for chunk in range(chunks):
            for m in range(MXUS):
                left = first_w[chunk * CHUNK : (chunk + 1) * CHUNK]
                pltpu.matmul_acc_lhs(accs[m][chunk], left, 0 if chunk == 0 else None)
            if chunk == 1 or chunk == 4:
                k = chunk // 4
                for m in range(MXUS):
                    right = hidden[other, k * depth : (k + 1) * depth, m * half : (m + 1) * half]
                    pltpu.matmul_push_rhs(right, k, m)
            if chunk >= 1:
                for m in range(MXUS):
                    take(slot, chunk - 1, m, variance)
        for k in range(hid // depth):
            for m in range(MXUS):
                pltpu.matmul_acc_lhs(accs[m][chunks], second_w[:, k * depth : (k + 1) * depth], k)
            if k == 0:
                push_pairs((group + 1) * GROUP)
        weigh((group - 2) * GROUP, slot)
        for m in range(MXUS):
            take(slot, chunks - 1, m, variance)
            spread_now = jnp.sum(variance[m], axis=0, keepdims=True) * (1.0 / width)
            spread[slot, :, m * half : (m + 1) * half] = jnp.broadcast_to(
                lax.rsqrt(spread_now + EPS), (8, half)
            )
            cols = slice(m * half, (m + 1) * half)
            scale = spread[other, :1, cols]
            change = pltpu.matmul_pop(accs[m][chunks])
            bias = jnp.concatenate([bias_tile[...]] * (half // 128), axis=1)
            values = direct[other, :, cols] + bias + jnp.where(scale > 0, scale * change, 0.0)
            logits[other, :, cols] = values

    groups = pl.cdiv(count, GROUP)

    def wait_for(g):
        for s in range(slots):

            @pl.when((metas[s][0] >= 0) & (starts[s] // batch == g))
            def _(s=s):
                slot_copy(s).wait()

    wait_for(0)
    push_pairs(0)

    def loop(g, carry):
        wait_for(g + 1)
        for u in range(UNROLL):
            stage(g * UNROLL + u, u % 2)
        return carry

    steps = pl.cdiv(groups + 2, UNROLL)
    lax.fori_loop(0, steps, loop, 0)
    for m in range(MXUS):
        pltpu.matmul_acc_lhs(accs[m][0], first_w[:CHUNK], 0)
        pltpu.matmul_pop(accs[m][0])
    for s in range(slots):

        @pl.when((metas[s][0] >= 0) & (starts[s] // batch > steps))
        def _(s=s):
            slot_copy(s).wait()

    for s in range(slots):
        member = jnp.maximum(metas[s][0], 0)
        block_row = jnp.maximum(metas[s][1], 0)
        block_col = jnp.maximum(metas[s][2], 0)
        row_ok = valid_row(resolved_ref, lengths_ref, member, block_row, side)
        col_ok = valid_row(resolved_ref, lengths_ref, member, block_col, side)
        outer = jnp.transpose(jnp.broadcast_to(row_ok, (side, side))) * col_ok
        rows = pl.ds(s * side, side)
        errors[s] = jnp.where(outer > 0, found_error[rows], 0.0)
        term = jnp.where(outer > 0, found_term[rows], 0.0)
        tm_row = jnp.sum(jnp.transpose(term), axis=0, keepdims=True)
        tm_sums[s] = jnp.broadcast_to(tm_row, (PAD, side))

    for shift in range(n_cplx):
        owner = lax.rem(cplx_index + shift, n_cplx)
        chosen = jnp.int32(0)
        for s in range(slots):
            hit = (metas[s][0] >= 0) & (metas[s][0] // cpx_dev == owner)
            chosen = jnp.where(hit, s, chosen)
        for part_shift in range(parts):
            part = lax.rem(part_index + part_shift, parts)
            out = outs[shift * parts + part_shift]
            first = pl.multiple_of(part * rows_each, rows_each)
            out[:rows_each] = errors[chosen, pl.ds(first, rows_each)]
            out[rows_each:] = tm_sums[chosen]


def head_kernel(dims, *refs):
    _, _, _, _, _, width, hid, bins, _ = dims
    chunks = (hid + bins + width) // CHUNK
    accs = [pltpu.ACC(m)((CHUNK, 2 * width), F32) for _ in range(chunks + 1) for m in range(MXUS)]
    pl.run_scoped(functools.partial(head_body, dims, *refs), *accs)


def place_kernel(dims, map_ref, *rest):
    n_cplx, parts, cpx_dev, slots, blocks, rows_each, side = dims
    pieces = rest[: n_cplx * parts]
    outs = rest[n_cplx * parts : n_cplx * parts + blocks]
    (tm_rows,) = rest[n_cplx * parts + blocks :]
    tile_index = lax.axis_index("tile")
    cplx_index = lax.axis_index("cplx")
    part_index = lax.rem(tile_index, parts)
    block_index = tile_index // parts
    body = cpx_dev * blocks * rows_each
    for out in outs:
        out[...] = jnp.zeros_like(out)
    tm_rows[...] = jnp.zeros_like(tm_rows)
    for shift in range(n_cplx):
        source = lax.rem(cplx_index + (n_cplx - shift), n_cplx)
        for part_shift in range(parts):
            part = lax.rem(part_index + (parts - part_shift), parts)
            device = (block_index * parts + part) * n_cplx + source
            piece = pieces[shift * parts + part_shift]
            member = jnp.int32(-1)
            block_row = jnp.int32(0)
            block_col = jnp.int32(0)
            for s, (k, r, q) in enumerate(own_slots(map_ref, device * slots, slots)):
                hit = (k >= 0) & (k // cpx_dev == cplx_index)
                member = jnp.where(hit, k - cplx_index * cpx_dev, member)
                block_row = jnp.where(hit, r, block_row)
                block_col = jnp.where(hit, q, block_col)
            offset = lax.rem(block_row - block_index + blocks, blocks)
            for b in range(blocks):

                @pl.when((member >= 0) & (offset == b))
                def _(b=b, piece=piece, member=member, block_col=block_col):
                    first = pl.multiple_of((member * blocks + block_col) * rows_each, 8)
                    outs[b][pl.ds(first, rows_each)] = piece[:rows_each]

            @pl.when(member >= 0)
            def _(piece=piece, member=member, block_row=block_row):
                row = member * blocks + block_row
                tm_rows[pl.ds(row, 1)] += piece[rows_each : rows_each + 1]

    for out in outs:
        out[body:] = tm_rows[...]


def finish_kernel(dims, lengths_ref, resolved_ref, *rest):
    parts, cpx_dev, blocks, rows_each, side = dims
    shares = rest[:blocks]
    map_out, error_out, score_out = rest[blocks:]
    tile_index = lax.axis_index("tile")
    cplx_index = lax.axis_index("cplx")
    part_index = lax.rem(tile_index, parts)
    block_index = tile_index // parts
    body = cpx_dev * blocks * rows_each
    tm_all = shares[0][body:]
    for share in shares[1:]:
        tm_all = tm_all + share[body:]
    for m in range(cpx_dev):
        member = cplx_index * cpx_dev + m
        masks = [valid_row(resolved_ref, lengths_ref, member, b, side) for b in range(blocks)]
        count = jnp.sum(functools.reduce(jnp.add, masks), axis=1, keepdims=True)
        row_sum = jnp.zeros((rows_each, side), F32)
        for q in range(blocks):
            rows = pl.ds((m * blocks + q) * rows_each, rows_each)
            block = shares[0][rows]
            for share in shares[1:]:
                block = block + share[rows]
            map_out[m, :, q * side : (q + 1) * side] = block
            row_sum = row_sum + block
        row_total = lax.dot_general(
            jnp.ones((8, side), F32), row_sum, NT, preferred_element_type=F32, precision=HIGHEST
        )[:1]
        best = jnp.zeros((1, side), F32)
        own_mask = jnp.zeros((1, side), F32)
        for b in range(blocks):
            denominator = jnp.maximum(masks[b] * count, 1.0)
            ratio = tm_all[m * blocks + b : m * blocks + b + 1] / denominator
            best = ratio if b == 0 else jnp.maximum(best, ratio)
            own_mask = jnp.where(block_index == b, masks[b], own_mask)
        own_mask = pltpu.roll(
            jnp.broadcast_to(own_mask, (8, side)),
            lax.rem(side - part_index * rows_each, side),
            axis=1,
        )[:1, :rows_each]
        error_out[m : m + 1, :] = row_total / jnp.maximum(own_mask * count, 1.0)
        score_out[m] = jnp.max(best)


def shards(pair_tiles, tile_map, lengths, resolved, ln_gain, w_in, w_out, w_head, head_bias):
    n_tile = lax.axis_size("tile")
    n_cplx = lax.axis_size("cplx")
    slots, side, _, width = pair_tiles.shape
    complexes, maxres = resolved.shape
    hid = w_in.shape[1]
    bins = w_head.shape[1]
    blocks = maxres // side
    cpx_dev = complexes // n_cplx
    rows_each = maxres // n_tile
    parts = side // rows_each
    smem = pl.BlockSpec(memory_space=pltpu.SMEM)
    vmem = pl.BlockSpec(memory_space=pltpu.VMEM)
    axes = ("tile", "cplx")
    lanes = GROUP * side

    def move(value, block_shift, part_shift, cplx_shift):
        pairs = []
        for t in range(n_tile):
            to_block = (t // parts + block_shift) % blocks
            to_part = (t % parts + part_shift) % parts
            for c in range(n_cplx):
                to = (to_block * parts + to_part) * n_cplx + (c + cplx_shift) % n_cplx
                pairs.append((t * n_cplx + c, to))
        return lax.ppermute(value, axes, pairs)

    piece = jax.ShapeDtypeStruct((rows_each + PAD, side), F32)
    pieces = pl.pallas_call(
        functools.partial(
            head_kernel, (n_cplx, parts, cpx_dev, slots, side, width, hid, bins, rows_each)
        ),
        out_shape=[piece] * (n_cplx * parts),
        in_specs=[smem, smem, smem, vmem, pl.BlockSpec(memory_space=pl.ANY)] + [vmem] * 5,
        out_specs=[vmem] * (n_cplx * parts),
        scratch_shapes=[
            pltpu.VMEM((slots * side + 8, side, width), BF16),
            pltpu.VMEM((hid + bins + width, 2 * width), BF16),
            pltpu.VMEM((bins, hid), BF16),
            pltpu.VMEM((bins, 128), F32),
            pltpu.VMEM((bins, 128), F32),
            pltpu.VMEM((slots + 1, bins, 128), F32),
            pltpu.VMEM((2, hid, lanes), BF16),
            pltpu.VMEM((2, bins, lanes), F32),
            pltpu.VMEM((2, 8, lanes), F32),
            pltpu.VMEM((2, bins, lanes), F32),
            pltpu.VMEM((slots * side + 8, side), F32),
            pltpu.VMEM((slots * side + 8, side), F32),
            pltpu.VMEM((slots, side, side), F32),
            pltpu.VMEM((slots, PAD, side), F32),
            pltpu.SMEM((slots * side + GROUP * (UNROLL + 4),), jnp.int32),
            pltpu.SemaphoreType.DMA((slots,)),
        ],
        compiler_params=pltpu.CompilerParams(vmem_limit_bytes=VMEM_LIMIT),
    )(
        tile_map.T,
        lengths,
        resolved,
        resolved,
        pair_tiles,
        ln_gain.reshape(1, width),
        w_in,
        w_out,
        w_head.T,
        head_bias.reshape(1, bins),
    )
    moved = []
    for shift in range(n_cplx):
        for part_shift in range(parts):
            value = pieces[shift * parts + part_shift]
            moved.append(move(value, 0, part_shift, shift) if shift or part_shift else value)

    tm_pad = -(-(cpx_dev * blocks) // 8) * 8
    share = jax.ShapeDtypeStruct((cpx_dev * blocks * rows_each + tm_pad, side), F32)
    shares = pl.pallas_call(
        functools.partial(
            place_kernel, (n_cplx, parts, cpx_dev, slots, blocks, rows_each, side)
        ),
        out_shape=[share] * blocks,
        in_specs=[smem] + [vmem] * len(moved),
        out_specs=[vmem] * blocks,
        scratch_shapes=[pltpu.VMEM((tm_pad, side), F32)],
        compiler_params=pltpu.CompilerParams(vmem_limit_bytes=VMEM_LIMIT),
    )(tile_map.T, *moved)
    arrived = [move(shares[b], b, 0, 0) if b else shares[b] for b in range(blocks)]

    return pl.pallas_call(
        functools.partial(finish_kernel, (parts, cpx_dev, blocks, rows_each, side)),
        out_shape=[
            jax.ShapeDtypeStruct((cpx_dev, rows_each, maxres), F32),
            jax.ShapeDtypeStruct((cpx_dev, rows_each), F32),
            jax.ShapeDtypeStruct((cpx_dev,), F32),
        ],
        in_specs=[smem, vmem] + [vmem] * blocks,
        out_specs=[vmem, vmem, smem],
        compiler_params=pltpu.CompilerParams(vmem_limit_bytes=VMEM_LIMIT),
    )(lengths, resolved, *arrived)


def solution(mesh):
    placed = (P(("tile", "cplx"), None, None, None), P(), P(), P(), P(), P(), P(), P(), P())
    return jax.shard_map(
        shards,
        mesh=mesh,
        in_specs=placed,
        out_specs=(P("cplx", "tile", None), P("cplx", "tile"), P("cplx")),
        check_vma=False,
    )
```

```python
import functools
import math

import jax
import jax.numpy as jnp
from jax import lax
from jax.experimental import pallas as pl
from jax.experimental.pallas import tpu as pltpu
from jax.sharding import PartitionSpec as P

EPS = 1e-05
F32 = jnp.float32
BF16 = jnp.bfloat16
LOG2E = math.log2(math.e)
NT = (((1,), (1,)), ((), ()))
HIGHEST = lax.Precision.HIGHEST
GROUP = 4
UNROLL = 4
MXUS = 2
CHUNK = 64
PAD = 8
VMEM_LIMIT = 67043328


def split_bf16(values):
    high = values.astype(BF16)
    return high, (values - high.astype(F32)).astype(BF16)


def own_slots(map_ref, base, slots):
    return [
        (map_ref[0, base + s], map_ref[1, base + s], map_ref[2, base + s]) for s in range(slots)
    ]


def valid_row(resolved_ref, lengths_ref, member, block, side):
    start = block * side
    if not isinstance(start, int):
        start = pl.multiple_of(start, side)
    flags = resolved_ref[:, pl.ds(start, side)]
    here = lax.broadcasted_iota(jnp.int32, flags.shape, 0) == member
    flags = jnp.max(jnp.where(here, flags, 0), axis=0, keepdims=True)
    position = start + lax.broadcasted_iota(jnp.int32, (1, side), 1)
    return ((flags > 0) & (position < lengths_ref[member])).astype(F32)


def head_body(
    dims,
    tiles_ref,
    *rest,
):
    n_cplx, parts, cpx_dev, slots, side, width, hid, bins, rows_each = dims
    operands, rest = rest[:8], rest[8:]
    outs = rest[: n_cplx * parts]
    (
        map_ref,
        lengths_ref,
        resolved_ref,
        gain_ref,
        w_in_ref,
        w_out_ref,
        w_head_ref,
        bias_ref,
        operand_sems,
        tiles,
        first_w,
        second_w,
        bias_tile,
        center_tile,
        tm_tile,
        hidden,
        direct,
        spread,
        logits,
        found_error,
        found_term,
        errors,
        tm_sums,
        order,
        sems,
        *accs,
    ) = rest[n_cplx * parts :]
    accs = [accs[m :: MXUS] for m in range(MXUS)]
    tile_index = lax.axis_index("tile")
    cplx_index = lax.axis_index("cplx")
    part_index = lax.rem(tile_index, parts)
    total = slots * side

    def slot_copy(s):
        return pltpu.make_async_copy(
            tiles_ref.at[s], tiles.at[pl.ds(s * side, side)], sems.at[s]
        )

    places = (
        map_ref, lengths_ref, resolved_ref, gain_ref, w_in_ref, w_out_ref, w_head_ref, bias_ref
    )
    loads = [
        pltpu.make_async_copy(source, place, operand_sems.at[n])
        for n, (source, place) in enumerate(zip(operands, places))
    ]
    for load in loads[:3]:
        load.start()
    slot_copy(0).start()
    for load in loads[3:]:
        load.start()
    for load in loads[:3]:
        load.wait()
    metas = own_slots(map_ref, (tile_index * n_cplx + cplx_index) * slots, slots)

    lane = lax.broadcasted_iota(jnp.int32, (1, side), 1)
    power = (1 << (lane & 15)).astype(F32)
    masks = []
    for s in range(slots):
        member = jnp.maximum(metas[s][0], 0)
        found = valid_row(resolved_ref, lengths_ref, member, jnp.maximum(metas[s][1], 0), side)
        found = jnp.where(metas[s][0] >= 0, found * power, 0.0)
        masks.append(
            [
                jnp.sum(jnp.where(lane // 16 == g, found, 0.0)).astype(jnp.int32)
                for g in range(side // 16)
            ]
        )
    count = jnp.int32(0)
    starts = []
    for s in range(slots):
        starts.append(count)
        for row in range(side):
            order[count] = s * side + row
            count = count + ((masks[s][row // 16] >> (row % 16)) & 1)
    batch = UNROLL * GROUP
    for u in range(4 * GROUP + batch):
        order[count + u] = total

    for load in loads[3:]:
        load.wait()
    w_in_t = jnp.transpose(w_in_ref[...].astype(F32)) * gain_ref[...]
    w_in_t = w_in_t - jnp.mean(w_in_t, axis=1, keepdims=True)
    head_t = w_head_ref[...].astype(F32)
    both = jnp.concatenate([w_in_t, head_t * LOG2E], axis=0)
    high, low = split_bf16(both)
    first_w[: hid + bins, :width] = high
    first_w[: hid + bins, width:] = low
    row_id = lax.broadcasted_iota(jnp.int32, (width, width), 0)
    col_id = lax.broadcasted_iota(jnp.int32, (width, width), 1)
    centring = jnp.where(row_id == col_id, 1.0, 0.0) - 1.0 / width
    first_w[hid + bins :, :width] = centring.astype(BF16)
    first_w[hid + bins :, width:] = jnp.zeros((width, width), BF16)
    left = jnp.concatenate([head_t, jnp.zeros_like(head_t)], axis=1).astype(BF16)
    for k in range(hid // (2 * width)):
        part = w_out_ref[k * 2 * width : (k + 1) * 2 * width]
        right = jnp.concatenate([part, jnp.zeros_like(part)], axis=1)
        pltpu.matmul_push_rhs(right, 0, k % MXUS, transpose=True)
        acc = accs[k % MXUS][0]
        pltpu.matmul_acc_lhs(acc, left, 0)
        second = pltpu.matmul_pop(acc) * LOG2E
        second_w[:, k * 2 * width : (k + 1) * 2 * width] = second.astype(BF16)
    bias_tile[...] = jnp.transpose(jnp.broadcast_to(bias_ref[...] * LOG2E, (128, bins)))
    step_size = 31.0 / (bins - 2)
    bin_id = lax.broadcasted_iota(jnp.int32, (bins, 128), 0)
    centers = (bin_id.astype(F32) + 0.5) * step_size
    center_tile[...] = centers
    for s in range(slots):
        length = lengths_ref[jnp.maximum(metas[s][0], 0)]
        clipped = jnp.full((bins, 128), jnp.maximum(length, 19) - 15, jnp.int32).astype(F32)
        distance = 1.24 * jnp.exp(jnp.log(clipped) * (1.0 / 3.0)) - 1.8
        tm_tile[s] = 1.0 / (1.0 + (centers / distance) ** 2)

    lanes = GROUP * side
    half = lanes // MXUS
    depth = 2 * width
    chunks = (hid + bins + width) // CHUNK

    def push_pairs(first_row):
        for m in range(MXUS):
            rows = [tiles[order[first_row + m * (GROUP // MXUS) + u]] for u in range(GROUP // MXUS)]
            pairs = jnp.concatenate(rows, axis=0)
            pairs = jnp.concatenate([pairs, pairs], axis=1)
            pltpu.matmul_push_rhs(pairs, 0, m, transpose=True)

    def measure(first_row, u, slot):
        values = jnp.transpose(tiles[order[first_row + u]]).astype(F32)
        centred = values - jnp.sum(values, axis=0, keepdims=True) * (1.0 / width)
        variance = jnp.sum(centred * centred, axis=0, keepdims=True) * (1.0 / width)
        spread[slot, :, u * side : (u + 1) * side] = jnp.broadcast_to(
            lax.rsqrt(variance + EPS), (8, side)
        )

    def take(slot, chunk, m, variance):
        value = pltpu.matmul_pop(accs[m][chunk])
        at = chunk * CHUNK
        cols = slice(m * half, (m + 1) * half)
        if at < hid:
            hidden[slot, at : at + CHUNK, cols] = jnp.maximum(value.astype(BF16), 0)
        elif at < hid + bins:
            direct[slot, at - hid : at - hid + CHUNK, cols] = value
        else:
            part = jnp.sum((value * value).reshape(CHUNK // 8, 8, half), axis=0)
            variance[m] = part if variance[m] is None else variance[m] + part

    def weigh(first_row, slot):
        for u in range(GROUP):
            row = order[jnp.maximum(first_row + u, 0)]
            row = jnp.where(first_row + u >= 0, row, total)
            values = logits[slot, :, u * side : (u + 1) * side]
            top = jnp.max(values, axis=0, keepdims=True)
            weights = jnp.exp2(values - top)
            inverse = 1.0 / jnp.sum(weights, axis=0, keepdims=True)
            expected = jnp.sum(weights * center_tile[...], axis=0, keepdims=True)
            term = jnp.sum(weights * tm_tile[row // side], axis=0, keepdims=True)
            found_error[pl.ds(row, 1)] = expected * inverse
            found_term[pl.ds(row, 1)] = term * inverse

    def stage(group, slot, direct_spread):
        other = 1 - slot
        variance = [None] * MXUS
        used = (hid + bins) // CHUNK if direct_spread else chunks
        for chunk in range(used):
            for m in range(MXUS):
                left = first_w[chunk * CHUNK : (chunk + 1) * CHUNK]
                pltpu.matmul_acc_lhs(accs[m][chunk], left, 0 if chunk == 0 else None)
            if chunk == 2 or chunk == 6:
                k = chunk // 6
                for m in range(MXUS):
                    right = hidden[other, k * depth : (k + 1) * depth, m * half : (m + 1) * half]
                    pltpu.matmul_push_rhs(right, k, m)
            if chunk >= 1:
                for m in range(MXUS):
                    take(slot, chunk - 1, m, variance)
            if direct_spread and chunk % 2 == 0 and chunk // 2 < GROUP:
                measure(group * GROUP, chunk // 2, slot)
        for k in range(hid // depth):
            for m in range(MXUS):
                pltpu.matmul_acc_lhs(accs[m][chunks], second_w[:, k * depth : (k + 1) * depth], k)
            if k == 0:
                push_pairs((group + 1) * GROUP)
        weigh((group - 2) * GROUP, slot)
        for m in range(MXUS):
            take(slot, used - 1, m, variance)
            cols = slice(m * half, (m + 1) * half)
            if not direct_spread:
                spread_now = jnp.sum(variance[m], axis=0, keepdims=True) * (1.0 / width)
                spread[slot, :, cols] = jnp.broadcast_to(lax.rsqrt(spread_now + EPS), (8, half))
            scale = spread[other, :1, cols]
            change = pltpu.matmul_pop(accs[m][chunks])
            bias = jnp.concatenate([bias_tile[...]] * (half // 128), axis=1)
            values = direct[other, :, cols] + bias + jnp.where(scale > 0, scale * change, 0.0)
            logits[other, :, cols] = values

    groups = pl.cdiv(count, GROUP)

    def wait_for(g):
        for s in range(1, slots):

            @pl.when(starts[s] // batch == g)
            def _(s=s):
                slot_copy(s).wait()

    slot_copy(0).wait()
    for s in range(1, slots):
        slot_copy(s).start()
    wait_for(0)
    push_pairs(0)

    def loop(g, carry):
        wait_for(g + 1)
        for u in range(UNROLL):
            stage(g * UNROLL + u, u % 2, True)
        return carry

    steps = pl.cdiv(groups + 2, UNROLL)
    lax.fori_loop(0, steps, loop, 0)
    for m in range(MXUS):
        pltpu.matmul_acc_lhs(accs[m][0], first_w[:CHUNK], 0)
        pltpu.matmul_pop(accs[m][0])
    for s in range(1, slots):

        @pl.when(starts[s] // batch > steps)
        def _(s=s):
            slot_copy(s).wait()

    for s in range(slots):
        member = jnp.maximum(metas[s][0], 0)
        block_row = jnp.maximum(metas[s][1], 0)
        block_col = jnp.maximum(metas[s][2], 0)
        row_ok = valid_row(resolved_ref, lengths_ref, member, block_row, side)
        col_ok = valid_row(resolved_ref, lengths_ref, member, block_col, side)
        outer = jnp.transpose(jnp.broadcast_to(row_ok, (side, side))) * col_ok
        rows = pl.ds(s * side, side)
        errors[s] = jnp.where(outer > 0, found_error[rows], 0.0)
        term = jnp.where(outer > 0, found_term[rows], 0.0)
        tm_row = jnp.sum(jnp.transpose(term), axis=0, keepdims=True)
        tm_sums[s] = jnp.broadcast_to(tm_row, (PAD, side))

    for shift in range(n_cplx):
        owner = lax.rem(cplx_index + shift, n_cplx)
        chosen = jnp.int32(0)
        for s in range(slots):
            hit = (metas[s][0] >= 0) & (metas[s][0] // cpx_dev == owner)
            chosen = jnp.where(hit, s, chosen)
        for part_shift in range(parts):
            part = lax.rem(part_index + part_shift, parts)
            out = outs[shift * parts + part_shift]
            first = pl.multiple_of(part * rows_each, rows_each)
            out[:rows_each] = errors[chosen, pl.ds(first, rows_each)]
            out[rows_each:] = tm_sums[chosen]


def head_kernel(dims, *refs):
    _, _, _, _, _, width, hid, bins, _ = dims
    chunks = (hid + bins + width) // CHUNK
    accs = [pltpu.ACC(m)((CHUNK, 2 * width), F32) for _ in range(chunks + 1) for m in range(MXUS)]
    pl.run_scoped(functools.partial(head_body, dims, *refs), *accs)


def place_kernel(dims, map_ref, *rest):
    n_cplx, parts, cpx_dev, slots, blocks, rows_each, side = dims
    pieces = rest[: n_cplx * parts]
    outs = rest[n_cplx * parts : n_cplx * parts + blocks]
    (tm_rows,) = rest[n_cplx * parts + blocks :]
    tile_index = lax.axis_index("tile")
    cplx_index = lax.axis_index("cplx")
    part_index = lax.rem(tile_index, parts)
    block_index = tile_index // parts
    body = cpx_dev * blocks * rows_each
    for out in outs:
        out[...] = jnp.zeros_like(out)
    tm_rows[...] = jnp.zeros_like(tm_rows)
    for shift in range(n_cplx):
        source = lax.rem(cplx_index + (n_cplx - shift), n_cplx)
        for part_shift in range(parts):
            part = lax.rem(part_index + (parts - part_shift), parts)
            device = (block_index * parts + part) * n_cplx + source
            piece = pieces[shift * parts + part_shift]
            member = jnp.int32(-1)
            block_row = jnp.int32(0)
            block_col = jnp.int32(0)
            for s, (k, r, q) in enumerate(own_slots(map_ref, device * slots, slots)):
                hit = (k >= 0) & (k // cpx_dev == cplx_index)
                member = jnp.where(hit, k - cplx_index * cpx_dev, member)
                block_row = jnp.where(hit, r, block_row)
                block_col = jnp.where(hit, q, block_col)
            offset = lax.rem(block_row - block_index + blocks, blocks)
            for b in range(blocks):

                @pl.when((member >= 0) & (offset == b))
                def _(b=b, piece=piece, member=member, block_col=block_col):
                    first = pl.multiple_of((member * blocks + block_col) * rows_each, 8)
                    outs[b][pl.ds(first, rows_each)] = piece[:rows_each]

            @pl.when(member >= 0)
            def _(piece=piece, member=member, block_row=block_row):
                row = member * blocks + block_row
                tm_rows[pl.ds(row, 1)] += piece[rows_each : rows_each + 1]

    for out in outs:
        out[body:] = tm_rows[...]


def finish_kernel(dims, lengths_ref, resolved_ref, *rest):
    parts, cpx_dev, blocks, rows_each, side = dims
    shares = rest[:blocks]
    map_out, error_out, score_out = rest[blocks:]
    tile_index = lax.axis_index("tile")
    cplx_index = lax.axis_index("cplx")
    part_index = lax.rem(tile_index, parts)
    block_index = tile_index // parts
    body = cpx_dev * blocks * rows_each
    tm_all = shares[0][body:]
    for share in shares[1:]:
        tm_all = tm_all + share[body:]
    for m in range(cpx_dev):
        member = cplx_index * cpx_dev + m
        masks = [valid_row(resolved_ref, lengths_ref, member, b, side) for b in range(blocks)]
        count = jnp.sum(functools.reduce(jnp.add, masks), axis=1, keepdims=True)
        row_sum = jnp.zeros((rows_each, side), F32)
        for q in range(blocks):
            rows = pl.ds((m * blocks + q) * rows_each, rows_each)
            block = shares[0][rows]
            for share in shares[1:]:
                block = block + share[rows]
            map_out[m, :, q * side : (q + 1) * side] = block
            row_sum = row_sum + block
        row_total = lax.dot_general(
            jnp.ones((8, side), F32), row_sum, NT, preferred_element_type=F32, precision=HIGHEST
        )[:1]
        best = jnp.zeros((1, side), F32)
        own_mask = jnp.zeros((1, side), F32)
        for b in range(blocks):
            denominator = jnp.maximum(masks[b] * count, 1.0)
            ratio = tm_all[m * blocks + b : m * blocks + b + 1] / denominator
            best = ratio if b == 0 else jnp.maximum(best, ratio)
            own_mask = jnp.where(block_index == b, masks[b], own_mask)
        own_mask = pltpu.roll(
            jnp.broadcast_to(own_mask, (8, side)),
            lax.rem(side - part_index * rows_each, side),
            axis=1,
        )[:1, :rows_each]
        error_out[m : m + 1, :] = row_total / jnp.maximum(own_mask * count, 1.0)
        score_out[m] = jnp.max(best)


def shards(pair_tiles, tile_map, lengths, resolved, ln_gain, w_in, w_out, w_head, head_bias):
    n_tile = lax.axis_size("tile")
    n_cplx = lax.axis_size("cplx")
    slots, side, _, width = pair_tiles.shape
    complexes, maxres = resolved.shape
    hid = w_in.shape[1]
    bins = w_head.shape[1]
    blocks = maxres // side
    cpx_dev = complexes // n_cplx
    rows_each = maxres // n_tile
    parts = side // rows_each
    smem = pl.BlockSpec(memory_space=pltpu.SMEM)
    vmem = pl.BlockSpec(memory_space=pltpu.VMEM)
    axes = ("tile", "cplx")
    lanes = GROUP * side

    def move(value, block_shift, part_shift, cplx_shift):
        pairs = []
        for t in range(n_tile):
            to_block = (t // parts + block_shift) % blocks
            to_part = (t % parts + part_shift) % parts
            for c in range(n_cplx):
                to = (to_block * parts + to_part) * n_cplx + (c + cplx_shift) % n_cplx
                pairs.append((t * n_cplx + c, to))
        return lax.ppermute(value, axes, pairs)

    piece = jax.ShapeDtypeStruct((rows_each + PAD, side), F32)
    pieces = pl.pallas_call(
        functools.partial(
            head_kernel, (n_cplx, parts, cpx_dev, slots, side, width, hid, bins, rows_each)
        ),
        out_shape=[piece] * (n_cplx * parts),
        in_specs=[pl.BlockSpec(memory_space=pl.ANY)] * 9,
        out_specs=[vmem] * (n_cplx * parts),
        scratch_shapes=[
            pltpu.SMEM(tile_map.shape[::-1], jnp.int32),
            pltpu.SMEM(lengths.shape, jnp.int32),
            pltpu.VMEM(resolved.shape, jnp.int32),
            pltpu.VMEM((1, width), F32),
            pltpu.VMEM(w_in.shape, BF16),
            pltpu.VMEM(w_out.shape, BF16),
            pltpu.VMEM(w_head.shape[::-1], BF16),
            pltpu.VMEM((1, bins), F32),
            pltpu.SemaphoreType.DMA((8,)),
            pltpu.VMEM((slots * side + 8, side, width), BF16),
            pltpu.VMEM((hid + bins + width, 2 * width), BF16),
            pltpu.VMEM((bins, hid), BF16),
            pltpu.VMEM((bins, 128), F32),
            pltpu.VMEM((bins, 128), F32),
            pltpu.VMEM((slots + 1, bins, 128), F32),
            pltpu.VMEM((2, hid, lanes), BF16),
            pltpu.VMEM((2, bins, lanes), F32),
            pltpu.VMEM((2, 8, lanes), F32),
            pltpu.VMEM((2, bins, lanes), F32),
            pltpu.VMEM((slots * side + 8, side), F32),
            pltpu.VMEM((slots * side + 8, side), F32),
            pltpu.VMEM((slots, side, side), F32),
            pltpu.VMEM((slots, PAD, side), F32),
            pltpu.SMEM((slots * side + GROUP * (UNROLL + 4),), jnp.int32),
            pltpu.SemaphoreType.DMA((slots,)),
        ],
        compiler_params=pltpu.CompilerParams(vmem_limit_bytes=VMEM_LIMIT),
    )(
        pair_tiles,
        tile_map.T,
        lengths,
        resolved,
        ln_gain.reshape(1, width),
        w_in,
        w_out,
        w_head.T,
        head_bias.reshape(1, bins),
    )
    moved = []
    for shift in range(n_cplx):
        for part_shift in range(parts):
            value = pieces[shift * parts + part_shift]
            moved.append(move(value, 0, part_shift, shift) if shift or part_shift else value)

    tm_pad = -(-(cpx_dev * blocks) // 8) * 8
    share = jax.ShapeDtypeStruct((cpx_dev * blocks * rows_each + tm_pad, side), F32)
    shares = pl.pallas_call(
        functools.partial(
            place_kernel, (n_cplx, parts, cpx_dev, slots, blocks, rows_each, side)
        ),
        out_shape=[share] * blocks,
        in_specs=[smem] + [vmem] * len(moved),
        out_specs=[vmem] * blocks,
        scratch_shapes=[pltpu.VMEM((tm_pad, side), F32)],
        compiler_params=pltpu.CompilerParams(vmem_limit_bytes=VMEM_LIMIT),
    )(tile_map.T, *moved)
    arrived = [move(shares[b], b, 0, 0) if b else shares[b] for b in range(blocks)]

    return pl.pallas_call(
        functools.partial(finish_kernel, (parts, cpx_dev, blocks, rows_each, side)),
        out_shape=[
            jax.ShapeDtypeStruct((cpx_dev, rows_each, maxres), F32),
            jax.ShapeDtypeStruct((cpx_dev, rows_each), F32),
            jax.ShapeDtypeStruct((cpx_dev,), F32),
        ],
        in_specs=[smem, vmem] + [vmem] * blocks,
        out_specs=[vmem, vmem, smem],
        compiler_params=pltpu.CompilerParams(vmem_limit_bytes=VMEM_LIMIT),
    )(lengths, resolved, *arrived)


def solution(mesh):
    placed = (P(("tile", "cplx"), None, None, None), P(), P(), P(), P(), P(), P(), P(), P())
    return jax.shard_map(
        shards,
        mesh=mesh,
        in_specs=placed,
        out_specs=(P("cplx", "tile", None), P("cplx", "tile"), P("cplx")),
        check_vma=False,
    )
```

```python
import functools
import math

import jax
import jax.numpy as jnp
from jax import lax
from jax.experimental import pallas as pl
from jax.experimental.pallas import tpu as pltpu
from jax.sharding import PartitionSpec as P

EPS = 1e-05
F32 = jnp.float32
BF16 = jnp.bfloat16
LOG2E = math.log2(math.e)
NT = (((1,), (1,)), ((), ()))
HIGHEST = lax.Precision.HIGHEST
GROUP = 4
UNROLL = 4
MXUS = 2
CHUNK = 64
PAD = 8
VMEM_LIMIT = 67043328


def split_bf16(values):
    high = values.astype(BF16)
    return high, (values - high.astype(F32)).astype(BF16)


def own_slots(map_ref, base, slots):
    return [
        (map_ref[0, base + s], map_ref[1, base + s], map_ref[2, base + s]) for s in range(slots)
    ]


def valid_row(resolved_ref, lengths_ref, member, block, side):
    start = block * side
    if not isinstance(start, int):
        start = pl.multiple_of(start, side)
    flags = resolved_ref[:, pl.ds(start, side)]
    here = lax.broadcasted_iota(jnp.int32, flags.shape, 0) == member
    flags = jnp.max(jnp.where(here, flags, 0), axis=0, keepdims=True)
    position = start + lax.broadcasted_iota(jnp.int32, (1, side), 1)
    return ((flags > 0) & (position < lengths_ref[member])).astype(F32)


def head_body(
    dims,
    tiles_ref,
    *rest,
):
    n_cplx, parts, cpx_dev, slots, side, width, hid, bins, rows_each = dims
    operands, rest = rest[:8], rest[8:]
    outs = rest[: n_cplx * parts]
    (
        map_ref,
        lengths_ref,
        resolved_ref,
        gain_ref,
        w_in_ref,
        w_out_ref,
        w_head_ref,
        bias_ref,
        operand_sems,
        tiles,
        first_w,
        second_w,
        bias_tile,
        center_tile,
        tm_tile,
        hidden,
        direct,
        spread,
        logits,
        found_error,
        found_term,
        errors,
        tm_sums,
        order,
        sems,
        *accs,
    ) = rest[n_cplx * parts :]
    accs = [accs[m :: MXUS] for m in range(MXUS)]
    tile_index = lax.axis_index("tile")
    cplx_index = lax.axis_index("cplx")
    part_index = lax.rem(tile_index, parts)
    total = slots * side

    def slot_copy(s):
        return pltpu.make_async_copy(
            tiles_ref.at[s], tiles.at[pl.ds(s * side, side)], sems.at[s]
        )

    places = (
        map_ref, lengths_ref, resolved_ref, gain_ref, w_in_ref, w_out_ref, w_head_ref, bias_ref
    )
    loads = [
        pltpu.make_async_copy(source, place, operand_sems.at[n])
        for n, (source, place) in enumerate(zip(operands, places))
    ]
    for load in loads[:3]:
        load.start()
    slot_copy(0).start()
    for load in loads[3:]:
        load.start()
    for load in loads[:3]:
        load.wait()
    metas = own_slots(map_ref, (tile_index * n_cplx + cplx_index) * slots, slots)

    lane = lax.broadcasted_iota(jnp.int32, (1, side), 1)
    power = (1 << (lane & 15)).astype(F32)
    masks = []
    for s in range(slots):
        member = jnp.maximum(metas[s][0], 0)
        found = valid_row(resolved_ref, lengths_ref, member, jnp.maximum(metas[s][1], 0), side)
        found = jnp.where(metas[s][0] >= 0, found * power, 0.0)
        masks.append(
            [
                jnp.sum(jnp.where(lane // 16 == g, found, 0.0)).astype(jnp.int32)
                for g in range(side // 16)
            ]
        )
    count = jnp.int32(0)
    starts = []
    for s in range(slots):
        starts.append(count)
        for row in range(side):
            order[count] = s * side + row
            count = count + ((masks[s][row // 16] >> (row % 16)) & 1)
    batch = UNROLL * GROUP
    for u in range(4 * GROUP + batch):
        order[count + u] = total

    for load in loads[3:]:
        load.wait()
    w_in_t = jnp.transpose(w_in_ref[...].astype(F32)) * gain_ref[...]
    w_in_t = w_in_t - jnp.mean(w_in_t, axis=1, keepdims=True)
    head_t = w_head_ref[...].astype(F32)
    both = jnp.concatenate([w_in_t, head_t * LOG2E], axis=0)
    high, low = split_bf16(both)
    first_w[: hid + bins, :width] = high
    first_w[: hid + bins, width:] = low
    row_id = lax.broadcasted_iota(jnp.int32, (width, width), 0)
    col_id = lax.broadcasted_iota(jnp.int32, (width, width), 1)
    centring = jnp.where(row_id == col_id, 1.0, 0.0) - 1.0 / width
    first_w[hid + bins :, :width] = centring.astype(BF16)
    first_w[hid + bins :, width:] = jnp.zeros((width, width), BF16)
    left = jnp.concatenate([head_t, jnp.zeros_like(head_t)], axis=1).astype(BF16)
    for k in range(hid // (2 * width)):
        part = w_out_ref[k * 2 * width : (k + 1) * 2 * width]
        right = jnp.concatenate([part, jnp.zeros_like(part)], axis=1)
        pltpu.matmul_push_rhs(right, 0, k % MXUS, transpose=True)
        acc = accs[k % MXUS][0]
        pltpu.matmul_acc_lhs(acc, left, 0)
        second = pltpu.matmul_pop(acc) * LOG2E
        second_w[:, k * 2 * width : (k + 1) * 2 * width] = second.astype(BF16)
    bias_tile[...] = jnp.transpose(jnp.broadcast_to(bias_ref[...] * LOG2E, (128, bins)))
    step_size = 31.0 / (bins - 2)
    bin_id = lax.broadcasted_iota(jnp.int32, (bins, 128), 0)
    centers = (bin_id.astype(F32) + 0.5) * step_size
    center_tile[...] = centers
    for s in range(slots):
        length = lengths_ref[jnp.maximum(metas[s][0], 0)]
        clipped = jnp.full((bins, 128), jnp.maximum(length, 19) - 15, jnp.int32).astype(F32)
        distance = 1.24 * jnp.exp(jnp.log(clipped) * (1.0 / 3.0)) - 1.8
        tm_tile[s] = 1.0 / (1.0 + (centers / distance) ** 2)

    lanes = GROUP * side
    half = lanes // MXUS
    depth = 2 * width
    chunks = (hid + bins + width) // CHUNK

    def push_pairs(first_row):
        for m in range(MXUS):
            rows = [tiles[order[first_row + m * (GROUP // MXUS) + u]] for u in range(GROUP // MXUS)]
            pairs = jnp.concatenate(rows, axis=0)
            pairs = jnp.concatenate([pairs, pairs], axis=1)
            pltpu.matmul_push_rhs(pairs, 0, m, transpose=True)

    def measure(first_row, u, slot):
        values = jnp.transpose(tiles[order[first_row + u]]).astype(F32)
        centred = values - jnp.sum(values, axis=0, keepdims=True) * (1.0 / width)
        variance = jnp.sum(centred * centred, axis=0, keepdims=True) * (1.0 / width)
        spread[slot, :, u * side : (u + 1) * side] = jnp.broadcast_to(
            lax.rsqrt(variance + EPS), (8, side)
        )

    def take(slot, chunk, m, variance):
        value = pltpu.matmul_pop(accs[m][chunk])
        at = chunk * CHUNK
        cols = slice(m * half, (m + 1) * half)
        if at < hid:
            hidden[slot, at : at + CHUNK, cols] = jnp.maximum(value.astype(BF16), 0)
        elif at < hid + bins:
            direct[slot, at - hid : at - hid + CHUNK, cols] = value
        else:
            part = jnp.sum((value * value).reshape(CHUNK // 8, 8, half), axis=0)
            variance[m] = part if variance[m] is None else variance[m] + part

    def weigh(first_row, slot):
        for u in range(GROUP):
            row = order[jnp.maximum(first_row + u, 0)]
            row = jnp.where(first_row + u >= 0, row, total)
            values = logits[slot, :, u * side : (u + 1) * side]
            top = jnp.max(values, axis=0, keepdims=True)
            weights = jnp.exp2(values - top)
            inverse = 1.0 / jnp.sum(weights, axis=0, keepdims=True)
            expected = jnp.sum(weights * center_tile[...], axis=0, keepdims=True)
            term = jnp.sum(weights * tm_tile[row // side], axis=0, keepdims=True)
            found_error[pl.ds(row, 1)] = expected * inverse
            found_term[pl.ds(row, 1)] = term * inverse

    def stage(group, slot, direct_spread):
        other = 1 - slot
        variance = [None] * MXUS
        used = (hid + bins) // CHUNK if direct_spread else chunks
        for chunk in range(used):
            for m in range(MXUS):
                left = first_w[chunk * CHUNK : (chunk + 1) * CHUNK]
                pltpu.matmul_acc_lhs(accs[m][chunk], left, 0 if chunk == 0 else None)
            if chunk == 3 or chunk == 7:
                k = chunk // 7
                for m in range(MXUS):
                    right = hidden[other, k * depth : (k + 1) * depth, m * half : (m + 1) * half]
                    pltpu.matmul_push_rhs(right, k, m)
            if chunk >= 1:
                for m in range(MXUS):
                    take(slot, chunk - 1, m, variance)
            if direct_spread and chunk % 2 == 0 and chunk // 2 < GROUP:
                measure(group * GROUP, chunk // 2, slot)
        for k in range(hid // depth):
            for m in range(MXUS):
                pltpu.matmul_acc_lhs(accs[m][chunks], second_w[:, k * depth : (k + 1) * depth], k)
            if k == 0:
                push_pairs((group + 1) * GROUP)
        weigh((group - 2) * GROUP, slot)
        for m in range(MXUS):
            take(slot, used - 1, m, variance)
            cols = slice(m * half, (m + 1) * half)
            if not direct_spread:
                spread_now = jnp.sum(variance[m], axis=0, keepdims=True) * (1.0 / width)
                spread[slot, :, cols] = jnp.broadcast_to(lax.rsqrt(spread_now + EPS), (8, half))
            scale = spread[other, :1, cols]
            change = pltpu.matmul_pop(accs[m][chunks])
            bias = jnp.concatenate([bias_tile[...]] * (half // 128), axis=1)
            values = direct[other, :, cols] + bias + jnp.where(scale > 0, scale * change, 0.0)
            logits[other, :, cols] = values

    groups = pl.cdiv(count, GROUP)

    def wait_for(g):
        for s in range(1, slots):

            @pl.when(starts[s] // batch == g)
            def _(s=s):
                slot_copy(s).wait()

    slot_copy(0).wait()
    for s in range(1, slots):
        slot_copy(s).start()
    wait_for(0)
    push_pairs(0)

    def loop(g, carry):
        wait_for(g + 1)
        for u in range(UNROLL):
            stage(g * UNROLL + u, u % 2, True)
        return carry

    steps = pl.cdiv(groups + 2, UNROLL)
    lax.fori_loop(0, steps, loop, 0)
    for m in range(MXUS):
        pltpu.matmul_acc_lhs(accs[m][0], first_w[:CHUNK], 0)
        pltpu.matmul_pop(accs[m][0])
    for s in range(1, slots):

        @pl.when(starts[s] // batch > steps)
        def _(s=s):
            slot_copy(s).wait()

    for s in range(slots):
        member = jnp.maximum(metas[s][0], 0)
        block_row = jnp.maximum(metas[s][1], 0)
        block_col = jnp.maximum(metas[s][2], 0)
        row_ok = valid_row(resolved_ref, lengths_ref, member, block_row, side)
        col_ok = valid_row(resolved_ref, lengths_ref, member, block_col, side)
        outer = jnp.transpose(jnp.broadcast_to(row_ok, (side, side))) * col_ok
        rows = pl.ds(s * side, side)
        errors[s] = jnp.where(outer > 0, found_error[rows], 0.0)
        term = jnp.where(outer > 0, found_term[rows], 0.0)
        tm_row = jnp.sum(jnp.transpose(term), axis=0, keepdims=True)
        tm_sums[s] = jnp.broadcast_to(tm_row, (PAD, side))

    for shift in range(n_cplx):
        owner = lax.rem(cplx_index + shift, n_cplx)
        chosen = jnp.int32(0)
        for s in range(slots):
            hit = (metas[s][0] >= 0) & (metas[s][0] // cpx_dev == owner)
            chosen = jnp.where(hit, s, chosen)
        for part_shift in range(parts):
            part = lax.rem(part_index + part_shift, parts)
            out = outs[shift * parts + part_shift]
            first = pl.multiple_of(part * rows_each, rows_each)
            out[:rows_each] = errors[chosen, pl.ds(first, rows_each)]
            out[rows_each:] = tm_sums[chosen]


def head_kernel(dims, *refs):
    _, _, _, _, _, width, hid, bins, _ = dims
    chunks = (hid + bins + width) // CHUNK
    accs = [pltpu.ACC(m)((CHUNK, 2 * width), F32) for _ in range(chunks + 1) for m in range(MXUS)]
    pl.run_scoped(functools.partial(head_body, dims, *refs), *accs)


def place_kernel(dims, map_ref, *rest):
    n_cplx, parts, cpx_dev, slots, blocks, rows_each, side = dims
    pieces = rest[: n_cplx * parts]
    outs = rest[n_cplx * parts : n_cplx * parts + blocks]
    (tm_rows,) = rest[n_cplx * parts + blocks :]
    tile_index = lax.axis_index("tile")
    cplx_index = lax.axis_index("cplx")
    part_index = lax.rem(tile_index, parts)
    block_index = tile_index // parts
    body = cpx_dev * blocks * rows_each
    for out in outs:
        out[...] = jnp.zeros_like(out)
    tm_rows[...] = jnp.zeros_like(tm_rows)
    for shift in range(n_cplx):
        source = lax.rem(cplx_index + (n_cplx - shift), n_cplx)
        for part_shift in range(parts):
            part = lax.rem(part_index + (parts - part_shift), parts)
            device = (block_index * parts + part) * n_cplx + source
            piece = pieces[shift * parts + part_shift]
            member = jnp.int32(-1)
            block_row = jnp.int32(0)
            block_col = jnp.int32(0)
            for s, (k, r, q) in enumerate(own_slots(map_ref, device * slots, slots)):
                hit = (k >= 0) & (k // cpx_dev == cplx_index)
                member = jnp.where(hit, k - cplx_index * cpx_dev, member)
                block_row = jnp.where(hit, r, block_row)
                block_col = jnp.where(hit, q, block_col)
            offset = lax.rem(block_row - block_index + blocks, blocks)
            for b in range(blocks):

                @pl.when((member >= 0) & (offset == b))
                def _(b=b, piece=piece, member=member, block_col=block_col):
                    first = pl.multiple_of((member * blocks + block_col) * rows_each, 8)
                    outs[b][pl.ds(first, rows_each)] = piece[:rows_each]

            @pl.when(member >= 0)
            def _(piece=piece, member=member, block_row=block_row):
                row = member * blocks + block_row
                tm_rows[pl.ds(row, 1)] += piece[rows_each : rows_each + 1]

    for out in outs:
        out[body:] = tm_rows[...]


def finish_kernel(dims, lengths_ref, resolved_ref, *rest):
    parts, cpx_dev, blocks, rows_each, side = dims
    shares = rest[:blocks]
    map_out, error_out, score_out = rest[blocks:]
    tile_index = lax.axis_index("tile")
    cplx_index = lax.axis_index("cplx")
    part_index = lax.rem(tile_index, parts)
    block_index = tile_index // parts
    body = cpx_dev * blocks * rows_each
    tm_all = shares[0][body:]
    for share in shares[1:]:
        tm_all = tm_all + share[body:]
    for m in range(cpx_dev):
        member = cplx_index * cpx_dev + m
        masks = [valid_row(resolved_ref, lengths_ref, member, b, side) for b in range(blocks)]
        count = jnp.sum(functools.reduce(jnp.add, masks), axis=1, keepdims=True)
        row_sum = jnp.zeros((rows_each, side), F32)
        for q in range(blocks):
            rows = pl.ds((m * blocks + q) * rows_each, rows_each)
            block = shares[0][rows]
            for share in shares[1:]:
                block = block + share[rows]
            map_out[m, :, q * side : (q + 1) * side] = block
            row_sum = row_sum + block
        row_total = lax.dot_general(
            jnp.ones((8, side), F32), row_sum, NT, preferred_element_type=F32, precision=HIGHEST
        )[:1]
        best = jnp.zeros((1, side), F32)
        own_mask = jnp.zeros((1, side), F32)
        for b in range(blocks):
            denominator = jnp.maximum(masks[b] * count, 1.0)
            ratio = tm_all[m * blocks + b : m * blocks + b + 1] / denominator
            best = ratio if b == 0 else jnp.maximum(best, ratio)
            own_mask = jnp.where(block_index == b, masks[b], own_mask)
        own_mask = pltpu.roll(
            jnp.broadcast_to(own_mask, (8, side)),
            lax.rem(side - part_index * rows_each, side),
            axis=1,
        )[:1, :rows_each]
        error_out[m : m + 1, :] = row_total / jnp.maximum(own_mask * count, 1.0)
        score_out[m] = jnp.max(best)


def shards(pair_tiles, tile_map, lengths, resolved, ln_gain, w_in, w_out, w_head, head_bias):
    n_tile = lax.axis_size("tile")
    n_cplx = lax.axis_size("cplx")
    slots, side, _, width = pair_tiles.shape
    complexes, maxres = resolved.shape
    hid = w_in.shape[1]
    bins = w_head.shape[1]
    blocks = maxres // side
    cpx_dev = complexes // n_cplx
    rows_each = maxres // n_tile
    parts = side // rows_each
    smem = pl.BlockSpec(memory_space=pltpu.SMEM)
    vmem = pl.BlockSpec(memory_space=pltpu.VMEM)
    axes = ("tile", "cplx")
    lanes = GROUP * side

    def move(value, block_shift, part_shift, cplx_shift):
        pairs = []
        for t in range(n_tile):
            to_block = (t // parts + block_shift) % blocks
            to_part = (t % parts + part_shift) % parts
            for c in range(n_cplx):
                to = (to_block * parts + to_part) * n_cplx + (c + cplx_shift) % n_cplx
                pairs.append((t * n_cplx + c, to))
        return lax.ppermute(value, axes, pairs)

    piece = jax.ShapeDtypeStruct((rows_each + PAD, side), F32)
    pieces = pl.pallas_call(
        functools.partial(
            head_kernel, (n_cplx, parts, cpx_dev, slots, side, width, hid, bins, rows_each)
        ),
        out_shape=[piece] * (n_cplx * parts),
        in_specs=[pl.BlockSpec(memory_space=pl.ANY)] * 9,
        out_specs=[vmem] * (n_cplx * parts),
        scratch_shapes=[
            pltpu.SMEM(tile_map.shape[::-1], jnp.int32),
            pltpu.SMEM(lengths.shape, jnp.int32),
            pltpu.VMEM(resolved.shape, jnp.int32),
            pltpu.VMEM((1, width), F32),
            pltpu.VMEM(w_in.shape, BF16),
            pltpu.VMEM(w_out.shape, BF16),
            pltpu.VMEM(w_head.shape[::-1], BF16),
            pltpu.VMEM((1, bins), F32),
            pltpu.SemaphoreType.DMA((8,)),
            pltpu.VMEM((slots * side + 8, side, width), BF16),
            pltpu.VMEM((hid + bins + width, 2 * width), BF16),
            pltpu.VMEM((bins, hid), BF16),
            pltpu.VMEM((bins, 128), F32),
            pltpu.VMEM((bins, 128), F32),
            pltpu.VMEM((slots + 1, bins, 128), F32),
            pltpu.VMEM((2, hid, lanes), BF16),
            pltpu.VMEM((2, bins, lanes), F32),
            pltpu.VMEM((2, 8, lanes), F32),
            pltpu.VMEM((2, bins, lanes), F32),
            pltpu.VMEM((slots * side + 8, side), F32),
            pltpu.VMEM((slots * side + 8, side), F32),
            pltpu.VMEM((slots, side, side), F32),
            pltpu.VMEM((slots, PAD, side), F32),
            pltpu.SMEM((slots * side + GROUP * (UNROLL + 4),), jnp.int32),
            pltpu.SemaphoreType.DMA((slots,)),
        ],
        compiler_params=pltpu.CompilerParams(vmem_limit_bytes=VMEM_LIMIT),
    )(
        pair_tiles,
        tile_map.T,
        lengths,
        resolved,
        ln_gain.reshape(1, width),
        w_in,
        w_out,
        w_head.T,
        head_bias.reshape(1, bins),
    )
    moved = []
    for shift in range(n_cplx):
        for part_shift in range(parts):
            value = pieces[shift * parts + part_shift]
            moved.append(move(value, 0, part_shift, shift) if shift or part_shift else value)

    tm_pad = -(-(cpx_dev * blocks) // 8) * 8
    share = jax.ShapeDtypeStruct((cpx_dev * blocks * rows_each + tm_pad, side), F32)
    shares = pl.pallas_call(
        functools.partial(
            place_kernel, (n_cplx, parts, cpx_dev, slots, blocks, rows_each, side)
        ),
        out_shape=[share] * blocks,
        in_specs=[smem] + [vmem] * len(moved),
        out_specs=[vmem] * blocks,
        scratch_shapes=[pltpu.VMEM((tm_pad, side), F32)],
        compiler_params=pltpu.CompilerParams(vmem_limit_bytes=VMEM_LIMIT),
    )(tile_map.T, *moved)
    arrived = [move(shares[b], b, 0, 0) if b else shares[b] for b in range(blocks)]

    return pl.pallas_call(
        functools.partial(finish_kernel, (parts, cpx_dev, blocks, rows_each, side)),
        out_shape=[
            jax.ShapeDtypeStruct((cpx_dev, rows_each, maxres), F32),
            jax.ShapeDtypeStruct((cpx_dev, rows_each), F32),
            jax.ShapeDtypeStruct((cpx_dev,), F32),
        ],
        in_specs=[smem, vmem] + [vmem] * blocks,
        out_specs=[vmem, vmem, smem],
        compiler_params=pltpu.CompilerParams(vmem_limit_bytes=VMEM_LIMIT),
    )(lengths, resolved, *arrived)


def solution(mesh):
    placed = (P(("tile", "cplx"), None, None, None), P(), P(), P(), P(), P(), P(), P(), P())
    return jax.shard_map(
        shards,
        mesh=mesh,
        in_specs=placed,
        out_specs=(P("cplx", "tile", None), P("cplx", "tile"), P("cplx")),
        check_vma=False,
    )
```
